128 devices in a mesh: dp: 16 (over x, y), tensor: 8 (over z, core).
Axes of the slice: x: 4, y: 4, z: 4, core: 2. Of those that a mesh axis runs over, the one named last changes fastest.
Arguments:
- inputs: bfloat16 [4096, 8192], P('dp', 'tensor'), may hold values from -6 to 6
- output_gradient: bfloat16 [4096, 8192], P('dp', 'tensor'), may hold values from -6 to 6
- frozen_weight: bfloat16 [8192, 8192], P(None, 'tensor'), may hold values from -0.0625 to 0.0625
- shrink_matrix_stack: bfloat16 [16, 8192, 64], P('dp', 'tensor'), may hold values from -0.0625 to 0.0625
- expand_matrix_stack: bfloat16 [16, 64, 8192], P('dp', None, 'tensor'), may hold values from -0.75 to 0.75
- adapter_index_rows: int32 [4096, 1], P('dp'), may hold values from 0 to 15; in each aligned block of 256 rows (0 to 255, 256 to 511, ...) at most 64 rows name the same one
- adapter_slot: int32 [16], replicated, may hold values from 0 to 15, each once
Outputs:
- projected_values: bfloat16 [4096, 8192], P('dp', 'tensor')
- activation_cotangent: bfloat16 [4096, 8192], P('dp', 'tensor')
- shrink_matrix_cotangent: bfloat16 [16, 8192, 64], P('dp', 'tensor')
- expand_matrix_cotangent: bfloat16 [16, 64, 8192], P('dp', None, 'tensor')
The draws below stay inside these ranges and needn't reach their ends.
Inputs may be any that keep to these rules, and one draw needn't show every extreme that they name: `adapter_index_rows`: among the rows of one index of dp no adapter is named more than 64 times, and in some of these blocks one adapter is named exactly 64 times. `adapter_slot`: each slot holds exactly one adapter; the slot s lies with dp index s.
All inputs are finite; a program needn't handle non-finite values.
Results may differ from the reference program's by a relative error of at most 0.022.
Values may be sent and summed in bfloat16 or wider, within the bound.
A program may use at most 128 MiB of HBM per device.

```python
import math
import jax
import jax.numpy as jnp
import numpy as np
from jax import lax

MODEL_WIDTH = 8192
ADAPTER_RANK = 64
TOK_DEV = 256
TOKENS = 4096
ADAPTER_TOTAL = 16
CAP = 64
N_TENSOR = 8


def level_of(rng, shape, split, smallest, largest):
    gain = 1.0
    for position, parts in split:
        draws = jax.random.uniform(jax.random.fold_in(jax.random.fold_in(rng, 6), position), (parts,), jnp.float32, smallest / len(split), largest / len(split))
        gain = gain * jnp.repeat(jnp.exp(draws), shape[position] // parts).reshape((-1,) + (1,) * (len(shape) - 1 - position))
    return gain


def assign_block(stream_key, own, number, rows, amount, top, reach, skew):
    sequence = jax.random.permutation(stream_key, amount)
    packed, usual = portions_of(amount, rows * top, reach, skew, True), portions_of(amount, rows * top, reach, skew, False)
    places = jnp.arange(amount)

    def named(tallies, turn):
        used = int((tallies > 0).sum())
        fixed = max(1, used // 4)
        passed = fixed + (places - fixed + turn * (used - fixed)) % max(1, amount - fixed)
        return jnp.zeros((amount,), jnp.int32).at[sequence[jnp.where(places < fixed, places, passed)]].set(jnp.asarray(tallies, jnp.int32))

    tallies = jnp.where(number % 4 == 0, named(packed, number // 4), named(usual, number - number // 4 - 1))
    mixed = jax.random.permutation(jax.random.fold_in(own, 3), amount)
    giver, taker = mixed[0:amount // 2 * 2:2], mixed[1:amount // 2 * 2:2]
    margin = jnp.minimum(tallies[giver] - 1, reach - tallies[taker]) // 2
    margin = jnp.where((giver == sequence[0]) | (taker == sequence[0]) | (tallies[taker] == 0), 0, jnp.maximum(margin, 0))
    passed = jax.random.randint(jax.random.fold_in(own, 4), (amount // 2,), 0, 1 << 20) % (margin + 1)
    tallies = tallies.at[giver].add(-passed).at[taker].add(passed)
    items = jnp.searchsorted(jnp.cumsum(tallies), jnp.arange(rows * top), side="right").astype(jnp.int32)
    table = items.reshape(top, rows).T
    table = table[jax.random.permutation(jax.random.fold_in(own, 1), rows)]
    turn = jax.random.randint(jax.random.fold_in(own, 2), (rows, 1), 0, top)
    return jnp.take_along_axis(table, (jnp.arange(top)[None, :] + turn) % top, axis=1)


def portions_of(count, total, most, skew, full):
    portions = [(1 << 20) // math.isqrt(standing ** skew) + 1 for standing in range(1, count + 1)]
    largest = most if full else min(most, max(-(-total // count), total * portions[0] // sum(portions)))
    least = 1 if total - largest >= count - 1 else 0
    counts, rest = [largest] + [least] * (count - 1), total - largest - least * (count - 1)
    while rest > 0:
        free = [i for i in range(1, count) if counts[i] < largest] or [i for i in range(1, count) if counts[i] < most]
        pool, remaining = sum([portions[i] for i in free]), rest
        for i in free:
            more = min(most - counts[i], max(1, remaining * portions[i] // pool), rest)
            counts[i] = counts[i] + more
            rest = rest - more
    return np.array(counts)


def bell_draw(rng, dims, width, limit, split=(), kind=jnp.bfloat16):
    drawn = jax.random.normal(rng, dims, jnp.float32) * width
    if len(split) > 0:
        drawn = level_of(rng, dims, split, -0.22, 0.18) * drawn
    return jnp.clip(drawn, min=-limit, max=limit).astype(kind)


def setup_inputs(seed: int = 0) -> dict:
    streams_of = jax.random.split(jax.random.key(seed), 8)
    inputs = bell_draw(streams_of[0], (TOKENS, MODEL_WIDTH), 1.0, 6.0, ((0, 16), (1, 8)))
    output_gradient = bell_draw(streams_of[1], (TOKENS, MODEL_WIDTH), 1.0, 6.0, ((0, 16), (1, 8)))
    frozen_weight = bell_draw(streams_of[2], (MODEL_WIDTH, MODEL_WIDTH), MODEL_WIDTH ** -0.5, 0.0625, ((1, 8),))
    shrink_matrix_stack = bell_draw(streams_of[3], (ADAPTER_TOTAL, MODEL_WIDTH, ADAPTER_RANK), MODEL_WIDTH ** -0.5, 0.0625, ((0, 16), (1, 8)))
    expand_matrix_stack = bell_draw(streams_of[4], (ADAPTER_TOTAL, ADAPTER_RANK, MODEL_WIDTH), ADAPTER_RANK ** -0.5, 0.75, ((0, 16), (2, 8)))
    adapter_index_rows_keys = jax.random.split(jax.random.fold_in(streams_of[5], 1), TOKENS // TOK_DEV)
    adapter_index_rows_turns = jax.random.permutation(jax.random.fold_in(streams_of[5], 3), TOKENS // TOK_DEV)
    adapter_index_rows = jax.vmap(lambda own, number: assign_block(jax.random.fold_in(streams_of[5], 2), own, number, TOK_DEV, ADAPTER_TOTAL, 1, CAP, 2))(adapter_index_rows_keys, adapter_index_rows_turns).reshape((TOKENS, 1))
    adapter_slot = jax.random.permutation(streams_of[6], ADAPTER_TOTAL).astype(jnp.int32)
    return {"inputs": inputs, "output_gradient": output_gradient, "frozen_weight": frozen_weight, "shrink_matrix_stack": shrink_matrix_stack, "expand_matrix_stack": expand_matrix_stack, "adapter_index_rows": adapter_index_rows, "adapter_slot": adapter_slot}


adapter_scale = 2.0


def reference(inputs, output_gradient, frozen_weight, shrink_matrix_stack, expand_matrix_stack, adapter_index_rows, adapter_slot):
    frozen_output = jnp.dot(inputs, frozen_weight, preferred_element_type=jnp.float32)
    block = MODEL_WIDTH // N_TENSOR
    frozen_backward = jnp.zeros((inputs.shape[0], MODEL_WIDTH), jnp.float32)
    for index in range(N_TENSOR):
        part = lax.dot_general(output_gradient[:, index * block:(index + 1) * block],
                               frozen_weight[:, index * block:(index + 1) * block],
                               (((1,), (1,)), ((), ())), preferred_element_type=jnp.float32)
        rounded = lax.optimization_barrier(part.astype(jnp.bfloat16))
        frozen_backward = frozen_backward + rounded.astype(jnp.float32)
    slot_position = adapter_slot[adapter_index_rows[:, 0]]

    def lone_entry_place(loop_carry, items):
        lowrank_delta_term, lowrank_reverse_pass = loop_carry
        number, down, upper_limit = items
        chosen = (slot_position == number)[:, None]
        reduced_hidden = jnp.dot(inputs, down, preferred_element_type=jnp.float32).astype(jnp.bfloat16)
        reduced_gradient = (adapter_scale * jnp.dot(output_gradient, upper_limit.T, preferred_element_type=jnp.float32)).astype(jnp.bfloat16)
        reduced_hidden = jnp.where(chosen, reduced_hidden, jnp.zeros_like(reduced_hidden))
        reduced_gradient = jnp.where(chosen, reduced_gradient, jnp.zeros_like(reduced_gradient))
        contribution = (adapter_scale * jnp.dot(reduced_hidden, upper_limit, preferred_element_type=jnp.float32)).astype(jnp.bfloat16)
        backward_result = jnp.dot(reduced_gradient, down.T, preferred_element_type=jnp.float32).astype(jnp.bfloat16)
        up_gradient_piece = (adapter_scale * jnp.dot(reduced_hidden.T, output_gradient, preferred_element_type=jnp.float32)).astype(jnp.bfloat16)
        down_gradient_piece = jnp.dot(inputs.T, reduced_gradient, preferred_element_type=jnp.float32).astype(jnp.bfloat16)
        return (lowrank_delta_term + contribution.astype(jnp.float32), lowrank_reverse_pass + backward_result.astype(jnp.float32)), (down_gradient_piece, up_gradient_piece)

    start_shift = (jnp.zeros((inputs.shape[0], MODEL_WIDTH), jnp.float32), jnp.zeros((inputs.shape[0], MODEL_WIDTH), jnp.float32))
    whole_number_run = jnp.arange(shrink_matrix_stack.shape[0], dtype=jnp.int32)
    (lowrank_delta_term, lowrank_reverse_pass), (shrink_matrix_cotangent, expand_matrix_cotangent) = lax.scan(lone_entry_place, start_shift, (whole_number_run, shrink_matrix_stack, expand_matrix_stack))
    projected_values = (frozen_output + lowrank_delta_term).astype(jnp.bfloat16)
    activation_cotangent = (frozen_backward + lowrank_reverse_pass).astype(jnp.bfloat16)
    return projected_values, activation_cotangent, shrink_matrix_cotangent, expand_matrix_cotangent
```

```python
import jax
import jax.numpy as jnp
from jax import lax
from jax.sharding import PartitionSpec as P

SCALE = 2.0
F32 = jnp.float32
BF16 = jnp.bfloat16


def dot(a, b, ca, cb):
    return lax.dot_general(a, b, (((ca,), (cb,)), ((), ())), preferred_element_type=F32)


def body(x, g, w, shrink, expand, index, table):
    rows = x.shape[0]
    slots = lax.axis_size("dp")
    rank = expand.shape[1]
    width = x.shape[1]
    ab = jnp.concatenate([shrink[0].T, expand[0]], axis=0)
    ab_all = lax.all_gather(ab, "dp", axis=0, tiled=False)
    x_all = lax.all_gather(x, "tensor", axis=1, tiled=True)
    back = dot(g, w, 1, 1).astype(BF16)
    base_back = lax.psum_scatter(back, "tensor", scatter_dimension=1, tiled=True)
    at_all = ab_all[:, :rank].reshape(slots * rank, width)
    b_all = ab_all[:, rank:].reshape(slots * rank, width)

    hit = index == jnp.arange(slots, dtype=jnp.int32)[None, :]
    slot = jnp.sum(jnp.where(hit, table[None, :], 0), axis=1)
    chosen = slot[:, None] == jnp.arange(slots, dtype=jnp.int32)[None, :]
    mask = jnp.repeat(chosen, rank, axis=1)

    def pick(full):
        return jnp.sum(jnp.where(mask, full, 0.0).reshape(rows, slots, rank), axis=1)

    part = jnp.concatenate([pick(dot(x, at_all, 1, 1)), pick(dot(g, b_all, 1, 1))], axis=1)
    both = lax.psum(part, "tensor")
    low = both[:, :rank].astype(BF16)
    low_grad = (SCALE * both[:, rank:]).astype(BF16)
    low_m = jnp.where(mask, jnp.tile(low, (1, slots)), 0).astype(BF16)
    grad_m = jnp.where(mask, jnp.tile(low_grad, (1, slots)), 0).astype(BF16)
    d_expand = (SCALE * dot(low_m, g, 0, 0)).astype(BF16).reshape(slots, rank, width)
    d_shrink = dot(grad_m, x, 0, 0).astype(BF16).reshape(slots, rank, width)
    d_both = lax.psum_scatter(
        jnp.concatenate([d_shrink, d_expand], axis=1), "dp", scatter_dimension=0, tiled=True
    )
    term = (SCALE * dot(low_m, b_all, 1, 0)).astype(BF16)
    back_term = dot(grad_m, at_all, 1, 0).astype(BF16)
    values = (dot(x_all, w, 1, 0) + term.astype(F32)).astype(BF16)
    cotangent = (base_back.astype(F32) + back_term.astype(F32)).astype(BF16)
    return values, cotangent, jnp.swapaxes(d_both[:, :rank], 1, 2), d_both[:, rank:]


def solution(mesh):
    return jax.shard_map(
        body,
        mesh=mesh,
        in_specs=(
            P("dp", "tensor"),
            P("dp", "tensor"),
            P(None, "tensor"),
            P("dp", "tensor", None),
            P("dp", None, "tensor"),
            P("dp", None),
            P(),
        ),
        out_specs=(
            P("dp", "tensor"),
            P("dp", "tensor"),
            P("dp", "tensor", None),
            P("dp", None, "tensor"),
        ),
        check_vma=False,
    )
```

```python
import jax
import jax.numpy as jnp
from jax import lax
from jax.experimental import pallas as pl
from jax.experimental.pallas import tpu as pltpu
from jax.sharding import PartitionSpec as P

SCALE = 2.0
F32 = jnp.float32
BF16 = jnp.bfloat16
MESH = pl.DeviceIdType.MESH
SIDE = 4
N_COPIES = 128
CHUNK = 256


def dot(a, b, ca, cb):
    return lax.dot_general(a, b, (((ca,), (cb,)), ((), ())), preferred_element_type=F32)


def chunks(width, step):
    def loop(n, carry):
        step(pl.ds(pl.multiple_of(n * CHUNK, CHUNK), CHUNK))
        return carry

    lax.fori_loop(0, width // CHUNK, loop, 0)


def kernel(
    x,
    g,
    w,
    at,
    b,
    index,
    table,
    values,
    cotangent,
    d_shrink,
    d_expand,
    wv,
    xs,
    buf_a,
    buf_b,
    part_a,
    part_b,
    psend,
    precv,
    ssum,
    z_half,
    z_full,
    acc,
    small,
    small_recv,
    small_sum,
    small_far,
    fin,
    lm_a,
    lm_b,
    r_half_a,
    r_half_b,
    r_full_a,
    r_full_b,
    red_a,
    red_b,
    t_half_a,
    t_half_b,
    t_full_a,
    t_full_b,
    wsem,
    send_sem,
    recv_sem,
):
    rows, width = x.shape
    rank = at.shape[0]
    half = rank // 2
    mid = rows // 2
    dp = lax.axis_index("dp")
    tensor = lax.axis_index("tensor")
    cx, cy = dp // SIDE, dp % SIDE
    cz, core = tensor // 2, tensor % 2

    def dev(dx=0, dy=0, dz=0, flip=0):
        to_x, to_y, to_z = (cx + dx) % SIDE, (cy + dy) % SIDE, (cz + dz) % SIDE
        to_core = 1 - core if flip else core
        return (to_x * SIDE + to_y, to_z * 2 + to_core)

    order = [(2, 1), (2, 0), (1, 1), (3, 1), (1, 0), (3, 0), (0, 1), (0, 0)]
    wcopies = {}
    for jz, jc in order:
        block = ((cz + jz) % SIDE) * 2 + (1 - core if jc else core)
        i = jz * 2 + jc
        wcopies[i] = pltpu.make_async_copy(
            w.at[pl.ds(pl.multiple_of(block * width, width), width), :], wv.at[i], wsem.at[i]
        )
        wcopies[i].start()

    barrier = pltpu.get_barrier_semaphore()
    peers = [dev(dx=1), dev(dx=3), dev(dy=1), dev(dy=3), dev(dz=1), dev(dz=2), dev(dz=3), dev(flip=1)]
    for peer in peers:
        pl.semaphore_signal(barrier, inc=1, device_id=peer, device_id_type=MESH)
    pl.semaphore_wait(barrier, len(peers))

    started = []

    def send(src, dst, to):
        n = len(started)
        copy = pltpu.make_async_remote_copy(
            src_ref=src,
            dst_ref=dst,
            send_sem=send_sem.at[n],
            recv_sem=recv_sem.at[n],
            device_id=to,
            device_id_type=MESH,
        )
        copy.start()
        started.append(copy)
        return copy

    lo, hi = pl.ds(0, half), pl.ds(half, half)
    pieces = (
        dict(
            own=at, buf=buf_a, part=part_a, f=lambda d: dev(dx=d), s=lambda d: dev(dy=d),
            slot=lambda jf, js: ((cx + jf) % SIDE) * SIDE + (cy + js) % SIDE,
            r_half=r_half_a, r_full=r_full_a, red=red_a, t_half=t_half_a, t_full=t_full_a,
            lm=lm_a, rhs=x, which=1, scale=1.0, out=d_shrink,
        ),
        dict(
            own=b, buf=buf_b, part=part_b, f=lambda d: dev(dy=d), s=lambda d: dev(dx=d),
            slot=lambda jf, js: ((cx + js) % SIDE) * SIDE + (cy + jf) % SIDE,
            r_half=r_half_b, r_full=r_full_b, red=red_b, t_half=t_half_b, t_full=t_full_b,
            lm=lm_b, rhs=g, which=0, scale=SCALE, out=d_expand,
        ),
    )

    def at_block(jf, js, sub=None):
        first = ((jf % SIDE) * SIDE + js % SIDE) * rank
        if sub is None:
            return pl.ds(first, rank)
        return pl.ds(first + sub * half, half)

    for p in pieces:
        p["c1"] = (
            send(p["own"], p["buf"].at[at_block(3, 0)], p["f"](1)),
            send(p["own"], p["buf"].at[at_block(1, 0)], p["f"](3)),
        )
    for p in pieces:
        p["d"] = {0: (
            send(p["own"], p["buf"].at[at_block(0, 3)], p["s"](1)),
            send(p["own"], p["buf"].at[at_block(0, 1)], p["s"](3)),
        )}
        p["e"] = {}
    top, bottom = pl.ds(0, mid), pl.ds(mid, mid)
    x_up = [send(x.at[top], xs.at[6, top], dev(dz=1))]
    x_down = [send(x.at[bottom], xs.at[2, bottom], dev(dz=3))]
    x_up.append(send(x.at[bottom], xs.at[6, bottom], dev(dz=1)))
    x_down.append(send(x.at[top], xs.at[2, top], dev(dz=3)))
    x_pair = [send(x, xs.at[1], dev(flip=1))]
    for p in pieces:
        p["buf"][at_block(0, 0), :] = p["own"][...]

    def forward_first(p):
        p["c1"][0].wait_recv()
        c2p = send(p["buf"].at[at_block(3, 0, 0)], p["buf"].at[at_block(2, 0, 0)], p["f"](1))
        p["c1"][1].wait_recv()
        c2m = send(p["buf"].at[at_block(1, 0, 1)], p["buf"].at[at_block(2, 0, 1)], p["f"](3))
        p["c2"] = (c2p, c2m)
        second(p, 3)
        second(p, 1)

    def second(p, jf):
        p["d"][jf] = (
            send(p["buf"].at[at_block(jf, 0)], p["buf"].at[at_block(jf, 3)], p["s"](1)),
            send(p["buf"].at[at_block(jf, 0)], p["buf"].at[at_block(jf, 1)], p["s"](3)),
        )

    def first_far(p):
        p["c2"][0].wait_recv()
        p["c2"][1].wait_recv()
        second(p, 2)

    def forward_second(p, jf):
        p["d"][jf][0].wait_recv()
        ep = send(p["buf"].at[at_block(jf, 3, 0)], p["buf"].at[at_block(jf, 2, 0)], p["s"](1))
        p["d"][jf][1].wait_recv()
        em = send(p["buf"].at[at_block(jf, 1, 1)], p["buf"].at[at_block(jf, 2, 1)], p["s"](3))
        p["e"][jf] = (ep, em)

    pair = {}

    def back_block(jz, jc):
        i = jz * 2 + jc
        wcopies[i].wait()
        target = psend if jc else ssum

        def step(cols):
            target[jz, :, cols] = dot(g[...], wv[i, cols, :], 1, 1).astype(BF16)

        chunks(width, step)
        if jc:
            pair[jz] = send(psend.at[jz], precv.at[jz], dev(flip=1))

    def pair_sum(jz):
        pair[jz].wait_recv()
        ssum[jz] = (ssum[jz].astype(F32) + precv[jz].astype(F32)).astype(BF16)

    def base_block(i, src, first=False):
        def step(cols):
            product = dot(src[...], wv[i, :, cols], 1, 0)
            acc[:, cols] = product if first else acc[:, cols] + product

        chunks(width, step)

    names = index[...]
    slot = jnp.zeros_like(names)
    for a in range(SIDE * SIDE):
        slot = jnp.where(names == a, table[a], slot)

    def project(p, jf, first=False):
        p["e"][jf][0].wait_recv()
        p["e"][jf][1].wait_recv()
        group = pl.ds(jf * SIDE * rank, SIDE * rank)
        full = dot(p["buf"][group, :], p["rhs"][...], 1, 1)
        total = jnp.zeros((rank, rows), F32) if first else small[p["which"]]
        for js in range(SIDE):
            own = full[js * rank : (js + 1) * rank, :]
            total = total + jnp.where(slot == p["slot"](jf, js), own, 0.0)
        small[p["which"]] = total

    project_a = dict(pieces[0], rhs=x, which=0)
    project_b = dict(pieces[1], rhs=g, which=1)

    back_block(2, 1)
    back_block(2, 0)
    for p in pieces:
        forward_first(p)
    back_block(1, 1)
    back_block(3, 1)
    pair_sum(2)
    z_first = (
        send(ssum.at[2, top], z_half.at[0], dev(dz=1)),
        send(ssum.at[2, bottom], z_half.at[1], dev(dz=3)),
    )
    for p in pieces:
        forward_second(p, 0)
    for p in pieces:
        first_far(p)
    back_block(1, 0)
    back_block(3, 0)
    pair_sum(1)
    pair_sum(3)
    x_up[0].wait_recv()
    x_far = [send(xs.at[6, top], xs.at[4, top], dev(dz=1))]
    x_down[0].wait_recv()
    x_far.append(send(xs.at[2, bottom], xs.at[4, bottom], dev(dz=3)))
    for p in pieces:
        forward_second(p, 3)
        forward_second(p, 1)
    back_block(0, 1)
    back_block(0, 0)
    base_block(0, x, first=True)
    project_a["e"], project_b["e"] = pieces[0]["e"], pieces[1]["e"]
    project(project_a, 0, first=True)
    project(project_b, 0, first=True)
    for p in pieces:
        forward_second(p, 2)
    x_pair[0].wait_recv()
    base_block(1, xs.at[1])
    x_up[1].wait_recv()
    x_pair.append(send(xs.at[6], xs.at[7], dev(flip=1)))
    x_down[1].wait_recv()
    x_pair.append(send(xs.at[2], xs.at[3], dev(flip=1)))
    for jf in (3, 1, 2):
        project(project_a, jf)
        project(project_b, jf)

    small_pair = send(small.at[1 - core], small_recv, dev(flip=1))
    base_block(6, xs.at[6])
    small_pair.wait_recv()
    small_sum[...] = small[core] + small_recv[...]
    far = [send(small_sum, small_far.at[3 - d], dev(dz=d)) for d in (1, 2, 3)]
    base_block(2, xs.at[2])
    for copy in far:
        copy.wait_recv()
    total = (small_sum[...] + small_far[0]) + (small_far[1] + small_far[2])
    fin[core] = (total * jnp.where(core == 1, SCALE, 1.0)).astype(BF16)
    small_pair = send(fin.at[core], fin.at[core], dev(flip=1))
    z_first[0].wait_recv()
    ssum[1, top] = (ssum[1, top].astype(F32) + z_half[0].astype(F32)).astype(BF16)
    z_second = [send(ssum.at[1], z_full.at[0], dev(dz=1))]
    z_first[1].wait_recv()
    ssum[3, bottom] = (ssum[3, bottom].astype(F32) + z_half[1].astype(F32)).astype(BF16)
    z_second.append(send(ssum.at[3], z_full.at[1], dev(dz=3)))
    small_pair.wait_recv()

    def partial(p, jf):
        low = fin[p["which"]]
        for js in range(SIDE):
            p["lm"][at_block(jf, js), :] = jnp.where(
                slot == p["slot"](jf, js), low.astype(F32), 0.0
            ).astype(BF16)
        group = pl.ds(jf * SIDE * rank, SIDE * rank)

        def step(cols):
            p["part"][group, cols] = (
                p["scale"] * dot(p["lm"][group, :], p["rhs"][:, cols], 1, 0)
            ).astype(BF16)

        chunks(width, step)
        p["rh"][jf] = (
            send(p["part"].at[at_block(jf, 2, 0)], p["r_half"].at[jf, 0], p["s"](1)),
            send(p["part"].at[at_block(jf, 2, 1)], p["r_half"].at[jf, 1], p["s"](3)),
        )

    def add_half(ref, where, addend):
        ref[where, :] = (ref[where, :].astype(F32) + addend.astype(F32)).astype(BF16)

    def reduce_second(p, jf):
        p["rh"][jf][0].wait_recv()
        add_half(p["part"], at_block(jf, 1, 0), p["r_half"][jf, 0])
        rp = send(p["part"].at[at_block(jf, 1)], p["r_full"].at[jf, 0], p["s"](1))
        p["rh"][jf][1].wait_recv()
        add_half(p["part"], at_block(jf, 3, 1), p["r_half"][jf, 1])
        rm = send(p["part"].at[at_block(jf, 3)], p["r_full"].at[jf, 1], p["s"](3))
        p["rf"][jf] = (rp, rm)

    def collected(p, jf):
        p["rf"][jf][0].wait_recv()
        p["rf"][jf][1].wait_recv()
        return (
            p["part"][at_block(jf, 0), :].astype(F32)
            + p["r_full"][jf, 0].astype(F32)
            + p["r_full"][jf, 1].astype(F32)
        )

    for p in pieces:
        p["rh"], p["rf"] = {}, {}
    for jf in (2, 1, 3, 0):
        for p in pieces:
            partial(p, jf)
    x_far[0].wait_recv()
    x_far[1].wait_recv()
    x_pair.append(send(xs.at[4], xs.at[5], dev(flip=1)))
    for p in pieces:
        reduce_second(p, 2)
    for p in pieces:
        reduce_second(p, 1)
    for p in pieces:
        reduce_second(p, 3)
    pair_sum(0)
    base_block(4, xs.at[4])
    x_pair[1].wait_recv()
    base_block(7, xs.at[7])
    x_pair[2].wait_recv()
    base_block(3, xs.at[3])
    for p in pieces:
        reduce_second(p, 0)
    for p in pieces:
        p["red"][0] = collected(p, 2).astype(BF16)
        p["th"] = (
            send(p["red"].at[0, lo], p["t_half"].at[0], p["f"](1)),
            send(p["red"].at[0, hi], p["t_half"].at[1], p["f"](3)),
        )
    x_pair[3].wait_recv()
    base_block(5, xs.at[5])

    def finish_values(cols):
        term = (SCALE * dot(lm_b[...], buf_b[:, cols], 0, 0)).astype(BF16)
        values[:, cols] = (acc[:, cols] + term.astype(F32)).astype(BF16)

    chunks(width, finish_values)
    for p in pieces:
        p["red"][1] = collected(p, 1).astype(BF16)
        p["red"][2] = collected(p, 3).astype(BF16)
    for p in pieces:
        p["th"][0].wait_recv()
        p["red"][1, lo] = (p["red"][1, lo].astype(F32) + p["t_half"][0].astype(F32)).astype(BF16)
        tp = send(p["red"].at[1], p["t_full"].at[0], p["f"](1))
        p["th"][1].wait_recv()
        p["red"][2, hi] = (p["red"][2, hi].astype(F32) + p["t_half"][1].astype(F32)).astype(BF16)
        tm = send(p["red"].at[2], p["t_full"].at[1], p["f"](3))
        p["tf"] = (tp, tm)
    z_second[0].wait_recv()
    z_second[1].wait_recv()

    def finish_cotangent(cols):
        term = dot(lm_a[...], buf_a[:, cols], 0, 0).astype(BF16)
        back = ssum[0, :, cols].astype(F32) + z_full[0, :, cols].astype(F32)
        back = back + z_full[1, :, cols].astype(F32)
        cotangent[:, cols] = (back + term.astype(F32)).astype(BF16)

    chunks(width, finish_cotangent)
    for p in pieces:
        own = collected(p, 0)
        p["tf"][0].wait_recv()
        p["tf"][1].wait_recv()
        p["out"][...] = (
            own + p["t_full"][0].astype(F32) + p["t_full"][1].astype(F32)
        ).astype(BF16)
    for copy in started:
        copy.wait_send()


def body(x, g, w, shrink, expand, index, table):
    rows, width = x.shape
    rank = expand.shape[1]
    slots = lax.axis_size("dp")
    vmem = pl.BlockSpec(memory_space=pltpu.VMEM)

    def scratch(*shape, dtype=BF16):
        return pltpu.VMEM(shape, dtype)

    out = pl.pallas_call(
        kernel,
        out_shape=(
            jax.ShapeDtypeStruct((rows, width), BF16),
            jax.ShapeDtypeStruct((rows, width), BF16),
            jax.ShapeDtypeStruct((rank, width), BF16),
            jax.ShapeDtypeStruct((rank, width), BF16),
        ),
        in_specs=[
            vmem,
            vmem,
            pl.BlockSpec(memory_space=pl.ANY),
            vmem,
            vmem,
            vmem,
            pl.BlockSpec(memory_space=pltpu.SMEM),
        ],
        out_specs=(vmem, vmem, vmem, vmem),
        scratch_shapes=[
            scratch(8, width, width),
            scratch(8, rows, width),
            scratch(slots * rank, width),
            scratch(slots * rank, width),
            scratch(slots * rank, width),
            scratch(slots * rank, width),
            scratch(4, rows, width),
            scratch(4, rows, width),
            scratch(4, rows, width),
            scratch(2, rows // 2, width),
            scratch(2, rows, width),
            scratch(rows, width, dtype=F32),
            scratch(2, rank, rows, dtype=F32),
            scratch(rank, rows, dtype=F32),
            scratch(rank, rows, dtype=F32),
            scratch(3, rank, rows, dtype=F32),
            scratch(2, rank, rows),
            scratch(slots * rank, rows),
            scratch(slots * rank, rows),
            scratch(4, 2, rank // 2, width),
            scratch(4, 2, rank // 2, width),
            scratch(4, 2, rank, width),
            scratch(4, 2, rank, width),
            scratch(3, rank, width),
            scratch(3, rank, width),
            scratch(2, rank // 2, width),
            scratch(2, rank // 2, width),
            scratch(2, rank, width),
            scratch(2, rank, width),
            pltpu.SemaphoreType.DMA((8,)),
            pltpu.SemaphoreType.DMA((N_COPIES,)),
            pltpu.SemaphoreType.DMA((N_COPIES,)),
        ],
        compiler_params=pltpu.CompilerParams(
            collective_id=0, has_side_effects=True, vmem_limit_bytes=60 * 1024 * 1024
        ),
    )(x, g, w, shrink[0].T, expand[0], index.reshape(1, rows), table)
    return out[0], out[1], out[2].T[None], out[3][None]


def solution(mesh):
    return jax.shard_map(
        body,
        mesh=mesh,
        in_specs=(
            P("dp", "tensor"),
            P("dp", "tensor"),
            P(None, "tensor"),
            P("dp", "tensor", None),
            P("dp", None, "tensor"),
            P("dp", None),
            P(),
        ),
        out_specs=(
            P("dp", "tensor"),
            P("dp", "tensor"),
            P("dp", "tensor", None),
            P("dp", None, "tensor"),
        ),
        check_vma=False,
    )
```

```python
import jax
import jax.numpy as jnp
from jax import lax
from jax.experimental import pallas as pl
from jax.experimental.pallas import tpu as pltpu
from jax.sharding import PartitionSpec as P

SCALE = 2.0
F32 = jnp.float32
BF16 = jnp.bfloat16
MESH = pl.DeviceIdType.MESH
SIDE = 4
N_COPIES = 128


def dot(a, b, ca, cb):
    return lax.dot_general(a, b, (((ca,), (cb,)), ((), ())), preferred_element_type=F32)


def chunks(width, step):
    step(pl.ds(0, width))


def kernel(
    x,
    g,
    w,
    at,
    b,
    index,
    table,
    values,
    cotangent,
    d_shrink,
    d_expand,
    wv,
    xs,
    buf_a,
    buf_b,
    part_a,
    part_b,
    psend,
    precv,
    ssum,
    z_half,
    z_full,
    acc,
    small,
    small_recv,
    small_sum,
    small_far,
    fin,
    lm_a,
    lm_b,
    r_half_a,
    r_half_b,
    r_full_a,
    r_full_b,
    red_a,
    red_b,
    t_half_a,
    t_half_b,
    t_full_a,
    t_full_b,
    wsem,
    send_sem,
    recv_sem,
):
    rows, width = x.shape
    rank = at.shape[0]
    half = rank // 2
    mid = rows // 2
    dp = lax.axis_index("dp")
    tensor = lax.axis_index("tensor")
    cx, cy = dp // SIDE, dp % SIDE
    cz, core = tensor // 2, tensor % 2

    def dev(dx=0, dy=0, dz=0, flip=0):
        to_x, to_y, to_z = (cx + dx) % SIDE, (cy + dy) % SIDE, (cz + dz) % SIDE
        to_core = 1 - core if flip else core
        return (to_x * SIDE + to_y, to_z * 2 + to_core)

    order = [(2, 1), (2, 0), (1, 1), (3, 1), (1, 0), (3, 0), (0, 1), (0, 0)]
    wcopies = {}
    for jz, jc in order:
        block = ((cz + jz) % SIDE) * 2 + (1 - core if jc else core)
        i = jz * 2 + jc
        wcopies[i] = pltpu.make_async_copy(
            w.at[pl.ds(pl.multiple_of(block * width, width), width), :], wv.at[i], wsem.at[i]
        )
        wcopies[i].start()

    barrier = pltpu.get_barrier_semaphore()
    peers = [dev(dx=1), dev(dx=3), dev(dy=1), dev(dy=3), dev(dz=1), dev(dz=2), dev(dz=3), dev(flip=1)]
    for peer in peers:
        pl.semaphore_signal(barrier, inc=1, device_id=peer, device_id_type=MESH)
    pl.semaphore_wait(barrier, len(peers))

    started = []

    def send(src, dst, to):
        n = len(started)
        copy = pltpu.make_async_remote_copy(
            src_ref=src,
            dst_ref=dst,
            send_sem=send_sem.at[n],
            recv_sem=recv_sem.at[n],
            device_id=to,
            device_id_type=MESH,
        )
        copy.start()
        started.append(copy)
        return copy

    lo, hi = pl.ds(0, half), pl.ds(half, half)
    pieces = (
        dict(
            own=at, buf=buf_a, part=part_a, f=lambda d: dev(dx=d), s=lambda d: dev(dy=d),
            slot=lambda jf, js: ((cx + jf) % SIDE) * SIDE + (cy + js) % SIDE,
            r_half=r_half_a, r_full=r_full_a, red=red_a, t_half=t_half_a, t_full=t_full_a,
            lm=lm_a, rhs=x, which=1, scale=1.0, out=d_shrink,
        ),
        dict(
            own=b, buf=buf_b, part=part_b, f=lambda d: dev(dy=d), s=lambda d: dev(dx=d),
            slot=lambda jf, js: ((cx + js) % SIDE) * SIDE + (cy + jf) % SIDE,
            r_half=r_half_b, r_full=r_full_b, red=red_b, t_half=t_half_b, t_full=t_full_b,
            lm=lm_b, rhs=g, which=0, scale=SCALE, out=d_expand,
        ),
    )

    def at_block(jf, js, sub=None):
        first = ((jf % SIDE) * SIDE + js % SIDE) * rank
        if sub is None:
            return pl.ds(first, rank)
        return pl.ds(first + sub * half, half)

    for p in pieces:
        p["c1"] = (
            send(p["own"], p["buf"].at[at_block(3, 0)], p["f"](1)),
            send(p["own"], p["buf"].at[at_block(1, 0)], p["f"](3)),
        )
    for p in pieces:
        p["d"] = {0: (
            send(p["own"], p["buf"].at[at_block(0, 3)], p["s"](1)),
            send(p["own"], p["buf"].at[at_block(0, 1)], p["s"](3)),
        )}
        p["e"] = {}
    top, bottom = pl.ds(0, mid), pl.ds(mid, mid)
    x_up = [send(x.at[top], xs.at[6, top], dev(dz=1))]
    x_down = [send(x.at[bottom], xs.at[2, bottom], dev(dz=3))]
    x_up.append(send(x.at[bottom], xs.at[6, bottom], dev(dz=1)))
    x_down.append(send(x.at[top], xs.at[2, top], dev(dz=3)))
    x_pair = [send(x, xs.at[1], dev(flip=1))]
    for p in pieces:
        p["buf"][at_block(0, 0), :] = p["own"][...]

    def forward_first(p):
        p["c1"][0].wait_recv()
        c2p = send(p["buf"].at[at_block(3, 0, 0)], p["buf"].at[at_block(2, 0, 0)], p["f"](1))
        p["c1"][1].wait_recv()
        c2m = send(p["buf"].at[at_block(1, 0, 1)], p["buf"].at[at_block(2, 0, 1)], p["f"](3))
        p["c2"] = (c2p, c2m)
        second(p, 3)
        second(p, 1)

    def second(p, jf):
        p["d"][jf] = (
            send(p["buf"].at[at_block(jf, 0)], p["buf"].at[at_block(jf, 3)], p["s"](1)),
            send(p["buf"].at[at_block(jf, 0)], p["buf"].at[at_block(jf, 1)], p["s"](3)),
        )

    def first_far(p):
        p["c2"][0].wait_recv()
        p["c2"][1].wait_recv()
        second(p, 2)

    def forward_second(p, jf):
        p["d"][jf][0].wait_recv()
        ep = send(p["buf"].at[at_block(jf, 3, 0)], p["buf"].at[at_block(jf, 2, 0)], p["s"](1))
        p["d"][jf][1].wait_recv()
        em = send(p["buf"].at[at_block(jf, 1, 1)], p["buf"].at[at_block(jf, 2, 1)], p["s"](3))
        p["e"][jf] = (ep, em)

    pair = {}

    def back_block(jz, jc):
        i = jz * 2 + jc
        wcopies[i].wait()
        target = psend if jc else ssum

        def step(cols):
            target[jz, :, cols] = dot(g[...], wv[i, cols, :], 1, 1).astype(BF16)

        chunks(width, step)
        if jc:
            pair[jz] = send(psend.at[jz], precv.at[jz], dev(flip=1))

    def pair_sum(jz):
        pair[jz].wait_recv()
        ssum[jz] = (ssum[jz].astype(F32) + precv[jz].astype(F32)).astype(BF16)

    def base_block(i, src, first=False):
        def step(cols):
            product = dot(src[...], wv[i, :, cols], 1, 0)
            acc[:, cols] = product if first else acc[:, cols] + product

        chunks(width, step)

    names = index[...]
    slot = jnp.zeros_like(names)
    for a in range(SIDE * SIDE):
        slot = jnp.where(names == a, table[a], slot)

    def project(p, jf, first=False):
        p["e"][jf][0].wait_recv()
        p["e"][jf][1].wait_recv()
        group = pl.ds(jf * SIDE * rank, SIDE * rank)
        full = dot(p["buf"][group, :], p["rhs"][...], 1, 1)
        total = jnp.zeros((rank, rows), F32) if first else small[p["which"]]
        for js in range(SIDE):
            own = full[js * rank : (js + 1) * rank, :]
            total = total + jnp.where(slot == p["slot"](jf, js), own, 0.0)
        small[p["which"]] = total

    project_a = dict(pieces[0], rhs=x, which=0)
    project_b = dict(pieces[1], rhs=g, which=1)

    back_block(2, 1)
    back_block(2, 0)
    for p in pieces:
        forward_first(p)
    back_block(1, 1)
    back_block(3, 1)
    pair_sum(2)
    z_first = (
        send(ssum.at[2, top], z_half.at[0], dev(dz=1)),
        send(ssum.at[2, bottom], z_half.at[1], dev(dz=3)),
    )
    for p in pieces:
        forward_second(p, 0)
    for p in pieces:
        first_far(p)
    back_block(1, 0)
    back_block(3, 0)
    pair_sum(1)
    pair_sum(3)
    x_up[0].wait_recv()
    x_far = [send(xs.at[6, top], xs.at[4, top], dev(dz=1))]
    x_down[0].wait_recv()
    x_far.append(send(xs.at[2, bottom], xs.at[4, bottom], dev(dz=3)))
    for p in pieces:
        forward_second(p, 3)
        forward_second(p, 1)
    back_block(0, 1)
    back_block(0, 0)
    base_block(0, x, first=True)
    project_a["e"], project_b["e"] = pieces[0]["e"], pieces[1]["e"]
    project(project_a, 0, first=True)
    project(project_b, 0, first=True)
    for p in pieces:
        forward_second(p, 2)
    x_pair[0].wait_recv()
    base_block(1, xs.at[1])
    x_up[1].wait_recv()
    x_pair.append(send(xs.at[6], xs.at[7], dev(flip=1)))
    x_down[1].wait_recv()
    x_pair.append(send(xs.at[2], xs.at[3], dev(flip=1)))
    for jf in (3, 1, 2):
        project(project_a, jf)
        project(project_b, jf)

    small_pair = send(small.at[1 - core], small_recv, dev(flip=1))
    base_block(6, xs.at[6])
    small_pair.wait_recv()
    small_sum[...] = small[core] + small_recv[...]
    far = [send(small_sum, small_far.at[3 - d], dev(dz=d)) for d in (1, 2, 3)]
    base_block(2, xs.at[2])
    for copy in far:
        copy.wait_recv()
    total = (small_sum[...] + small_far[0]) + (small_far[1] + small_far[2])
    fin[core] = (total * jnp.where(core == 1, SCALE, 1.0)).astype(BF16)
    small_pair = send(fin.at[core], fin.at[core], dev(flip=1))
    z_first[0].wait_recv()
    ssum[1, top] = (ssum[1, top].astype(F32) + z_half[0].astype(F32)).astype(BF16)
    z_second = [send(ssum.at[1], z_full.at[0], dev(dz=1))]
    z_first[1].wait_recv()
    ssum[3, bottom] = (ssum[3, bottom].astype(F32) + z_half[1].astype(F32)).astype(BF16)
    z_second.append(send(ssum.at[3], z_full.at[1], dev(dz=3)))
    small_pair.wait_recv()

    def partial(p, jf):
        low = fin[p["which"]]
        for js in range(SIDE):
            p["lm"][at_block(jf, js), :] = jnp.where(
                slot == p["slot"](jf, js), low.astype(F32), 0.0
            ).astype(BF16)
        group = pl.ds(jf * SIDE * rank, SIDE * rank)

        def step(cols):
            p["part"][group, cols] = (
                p["scale"] * dot(p["lm"][group, :], p["rhs"][:, cols], 1, 0)
            ).astype(BF16)

        chunks(width, step)
        p["rh"][jf] = (
            send(p["part"].at[at_block(jf, 2, 0)], p["r_half"].at[jf, 0], p["s"](1)),
            send(p["part"].at[at_block(jf, 2, 1)], p["r_half"].at[jf, 1], p["s"](3)),
        )

    def add_half(ref, where, addend):
        ref[where, :] = (ref[where, :].astype(F32) + addend.astype(F32)).astype(BF16)

    def reduce_second(p, jf):
        p["rh"][jf][0].wait_recv()
        add_half(p["part"], at_block(jf, 1, 0), p["r_half"][jf, 0])
        rp = send(p["part"].at[at_block(jf, 1)], p["r_full"].at[jf, 0], p["s"](1))
        p["rh"][jf][1].wait_recv()
        add_half(p["part"], at_block(jf, 3, 1), p["r_half"][jf, 1])
        rm = send(p["part"].at[at_block(jf, 3)], p["r_full"].at[jf, 1], p["s"](3))
        p["rf"][jf] = (rp, rm)

    def collected(p, jf):
        p["rf"][jf][0].wait_recv()
        p["rf"][jf][1].wait_recv()
        return (
            p["part"][at_block(jf, 0), :].astype(F32)
            + p["r_full"][jf, 0].astype(F32)
            + p["r_full"][jf, 1].astype(F32)
        )

    for p in pieces:
        p["rh"], p["rf"] = {}, {}
    for jf in (2, 1, 3, 0):
        for p in pieces:
            partial(p, jf)
    x_far[0].wait_recv()
    x_far[1].wait_recv()
    x_pair.append(send(xs.at[4], xs.at[5], dev(flip=1)))
    for p in pieces:
        reduce_second(p, 2)
    for p in pieces:
        reduce_second(p, 1)
    for p in pieces:
        reduce_second(p, 3)
    pair_sum(0)
    base_block(4, xs.at[4])
    x_pair[1].wait_recv()
    base_block(7, xs.at[7])
    x_pair[2].wait_recv()
    base_block(3, xs.at[3])
    for p in pieces:
        reduce_second(p, 0)
    for p in pieces:
        p["red"][0] = collected(p, 2).astype(BF16)
        p["th"] = (
            send(p["red"].at[0, lo], p["t_half"].at[0], p["f"](1)),
            send(p["red"].at[0, hi], p["t_half"].at[1], p["f"](3)),
        )
    x_pair[3].wait_recv()
    base_block(5, xs.at[5])

    def finish_values(cols):
        term = (SCALE * dot(lm_b[...], buf_b[:, cols], 0, 0)).astype(BF16)
        values[:, cols] = (acc[:, cols] + term.astype(F32)).astype(BF16)

    chunks(width, finish_values)
    for p in pieces:
        p["red"][1] = collected(p, 1).astype(BF16)
        p["red"][2] = collected(p, 3).astype(BF16)
    for p in pieces:
        p["th"][0].wait_recv()
        p["red"][1, lo] = (p["red"][1, lo].astype(F32) + p["t_half"][0].astype(F32)).astype(BF16)
        tp = send(p["red"].at[1], p["t_full"].at[0], p["f"](1))
        p["th"][1].wait_recv()
        p["red"][2, hi] = (p["red"][2, hi].astype(F32) + p["t_half"][1].astype(F32)).astype(BF16)
        tm = send(p["red"].at[2], p["t_full"].at[1], p["f"](3))
        p["tf"] = (tp, tm)
    z_second[0].wait_recv()
    z_second[1].wait_recv()

    def finish_cotangent(cols):
        term = dot(lm_a[...], buf_a[:, cols], 0, 0).astype(BF16)
        back = ssum[0, :, cols].astype(F32) + z_full[0, :, cols].astype(F32)
        back = back + z_full[1, :, cols].astype(F32)
        cotangent[:, cols] = (back + term.astype(F32)).astype(BF16)

    chunks(width, finish_cotangent)
    for p in pieces:
        own = collected(p, 0)
        p["tf"][0].wait_recv()
        p["tf"][1].wait_recv()
        p["out"][...] = (
            own + p["t_full"][0].astype(F32) + p["t_full"][1].astype(F32)
        ).astype(BF16)
    for copy in started:
        copy.wait_send()


def copy_out(*refs):
    half = len(refs) // 2
    sems = refs[-1]
    copies = [
        pltpu.make_async_copy(refs[i], refs[half + i], sems.at[i]) for i in range(half)
    ]
    for copy in copies:
        copy.start()
    for copy in copies:
        copy.wait()


def body(x, g, w, shrink, expand, index, table):
    rows, width = x.shape
    rank = expand.shape[1]
    slots = lax.axis_size("dp")
    vmem = pl.BlockSpec(memory_space=pltpu.VMEM)

    def scratch(*shape, dtype=BF16):
        return pltpu.VMEM(shape, dtype)

    out = pl.pallas_call(
        kernel,
        out_shape=(
            pltpu.VMEM((rows, width), BF16),
            pltpu.VMEM((rows, width), BF16),
            pltpu.VMEM((rank, width), BF16),
            pltpu.VMEM((rank, width), BF16),
        ),
        in_specs=[
            vmem,
            vmem,
            pl.BlockSpec(memory_space=pl.ANY),
            vmem,
            vmem,
            vmem,
            pl.BlockSpec(memory_space=pltpu.SMEM),
        ],
        out_specs=(vmem, vmem, vmem, vmem),
        scratch_shapes=[
            scratch(8, width, width),
            scratch(8, rows, width),
            scratch(slots * rank, width),
            scratch(slots * rank, width),
            scratch(slots * rank, width),
            scratch(slots * rank, width),
            scratch(4, rows, width),
            scratch(4, rows, width),
            scratch(4, rows, width),
            scratch(2, rows // 2, width),
            scratch(2, rows, width),
            scratch(rows, width, dtype=F32),
            scratch(2, rank, rows, dtype=F32),
            scratch(rank, rows, dtype=F32),
            scratch(rank, rows, dtype=F32),
            scratch(3, rank, rows, dtype=F32),
            scratch(2, rank, rows),
            scratch(slots * rank, rows),
            scratch(slots * rank, rows),
            scratch(4, 2, rank // 2, width),
            scratch(4, 2, rank // 2, width),
            scratch(4, 2, rank, width),
            scratch(4, 2, rank, width),
            scratch(3, rank, width),
            scratch(3, rank, width),
            scratch(2, rank // 2, width),
            scratch(2, rank // 2, width),
            scratch(2, rank, width),
            scratch(2, rank, width),
            pltpu.SemaphoreType.DMA((8,)),
            pltpu.SemaphoreType.DMA((N_COPIES,)),
            pltpu.SemaphoreType.DMA((N_COPIES,)),
        ],
        compiler_params=pltpu.CompilerParams(
            collective_id=0, has_side_effects=True, vmem_limit_bytes=56 * 1024 * 1024
        ),
    )(x, g, w, shrink[0].T, expand[0], index.reshape(1, rows), table)
    anywhere = pl.BlockSpec(memory_space=pl.ANY)
    out = pl.pallas_call(
        copy_out,
        out_shape=[jax.ShapeDtypeStruct(o.shape, o.dtype) for o in out],
        in_specs=[vmem] * 4,
        out_specs=[anywhere] * 4,
        scratch_shapes=[pltpu.SemaphoreType.DMA((4,))],
    )(*[pltpu.with_memory_space_constraint(o, pltpu.VMEM) for o in out])
    return out[0], out[1], out[2].T[None], out[3][None]


def solution(mesh):
    return jax.shard_map(
        body,
        mesh=mesh,
        in_specs=(
            P("dp", "tensor"),
            P("dp", "tensor"),
            P(None, "tensor"),
            P("dp", "tensor", None),
            P("dp", None, "tensor"),
            P("dp", None),
            P(),
        ),
        out_specs=(
            P("dp", "tensor"),
            P("dp", "tensor"),
            P("dp", "tensor", None),
            P("dp", None, "tensor"),
        ),
        check_vma=False,
    )
```

```python
import jax
import jax.numpy as jnp
from jax import lax
from jax.experimental import pallas as pl
from jax.experimental.pallas import tpu as pltpu
from jax.sharding import PartitionSpec as P

SCALE = 2.0
F32 = jnp.float32
BF16 = jnp.bfloat16
MESH = pl.DeviceIdType.MESH
SIDE = 4
N_COPIES = 160


def dot(a, b, ca, cb):
    return lax.dot_general(a, b, (((ca,), (cb,)), ((), ())), preferred_element_type=F32)


def kernel(
    x,
    g,
    w,
    at,
    b,
    index,
    table,
    values,
    cotangent,
    d_shrink,
    d_expand,
    wv,
    xs,
    buf,
    part,
    psend,
    precv,
    ssum,
    z_half,
    z_full,
    acc,
    small,
    small_recv,
    small_sum,
    small_far,
    fin,
    lm,
    r_half,
    r_full,
    red,
    t_half,
    t_full,
    wsem,
    send_sem,
    recv_sem,
):
    rows, width = x.shape
    rank = at.shape[0]
    half = rank // 2
    mid = rows // 2
    piece_rows = SIDE * SIDE * half
    dp = lax.axis_index("dp")
    tensor = lax.axis_index("tensor")
    cx, cy = dp // SIDE, dp % SIDE
    cz, core = tensor // 2, tensor % 2

    def dev(dx=0, dy=0, dz=0, flip=0):
        to_x, to_y, to_z = (cx + dx) % SIDE, (cy + dy) % SIDE, (cz + dz) % SIDE
        to_core = 1 - core if flip else core
        return (to_x * SIDE + to_y, to_z * 2 + to_core)

    order = [(2, 1), (2, 0), (1, 1), (3, 1), (1, 0), (3, 0), (0, 1), (0, 0)]
    wcopies = {}
    for jz, jc in order:
        block = ((cz + jz) % SIDE) * 2 + (1 - core if jc else core)
        i = jz * 2 + jc
        wcopies[i] = pltpu.make_async_copy(
            w.at[pl.ds(pl.multiple_of(block * width, width), width), :], wv.at[i], wsem.at[i]
        )
        wcopies[i].start()

    barrier = pltpu.get_barrier_semaphore()
    peers = [dev(dx=1), dev(dx=3), dev(dy=1), dev(dy=3), dev(dz=1), dev(dz=2), dev(dz=3), dev(flip=1)]
    for peer in peers:
        pl.semaphore_signal(barrier, inc=1, device_id=peer, device_id_type=MESH)
    pl.semaphore_wait(barrier, len(peers))

    started = []

    def send(src, dst, to):
        n = len(started)
        copy = pltpu.make_async_remote_copy(
            src_ref=src,
            dst_ref=dst,
            send_sem=send_sem.at[n],
            recv_sem=recv_sem.at[n],
            device_id=to,
            device_id_type=MESH,
        )
        copy.start()
        started.append(copy)
        return copy

    along_x, along_y = (lambda d: dev(dx=d)), (lambda d: dev(dy=d))
    pieces = []
    for i in range(4):
        x_first = i % 2 == 0
        pieces.append(
            dict(
                own=(at, b)[i // 2].at[pl.ds((i % 2) * half, half)],
                base=i * piece_rows,
                f=along_x if x_first else along_y,
                s=along_y if x_first else along_x,
                x_first=x_first,
                turn=1 if i < 2 else 3,
                i=i,
            )
        )
    turn_of = {0: 1, 1: 1, 2: 3, 3: 3}

    def slot_of(p, jf, js):
        jx, jy = (jf, js) if p["x_first"] else (js, jf)
        return ((cx + jx) % SIDE) * SIDE + (cy + jy) % SIDE

    def at_block(p, jf, js):
        return pl.ds(p["base"] + (jf * SIDE + js) * half, half)

    def own_sends(p):
        p["c"] = {
            1: send(p["own"], buf.at[at_block(p, 3, 0)], p["f"](1)),
            3: send(p["own"], buf.at[at_block(p, 1, 0)], p["f"](3)),
        }
        p["d"] = {0: {
            1: send(p["own"], buf.at[at_block(p, 0, 3)], p["s"](1)),
            3: send(p["own"], buf.at[at_block(p, 0, 1)], p["s"](3)),
        }}
        p["e"] = {}

    def keep_own(p):
        buf[at_block(p, 0, 0), :] = p["own"][...]

    def second(p, jf):
        src = buf.at[at_block(p, jf, 0)]
        p["d"][jf] = {
            1: send(src, buf.at[at_block(p, jf, 3)], p["s"](1)),
            3: send(src, buf.at[at_block(p, jf, 1)], p["s"](3)),
        }

    def forward_first(p):
        turn = p["turn"]
        p["c"][turn].wait_recv()
        near = 4 - turn
        p["c2"] = send(buf.at[at_block(p, near, 0)], buf.at[at_block(p, 2, 0)], p["f"](turn))
        second(p, near)
        p["c"][near].wait_recv()
        second(p, turn)

    def first_far(p):
        p["c2"].wait_recv()
        second(p, 2)

    def forward_second(p, jf):
        turn = turn_of[jf]
        p["d"][jf][turn].wait_recv()
        near = 4 - turn
        p["e"][jf] = send(buf.at[at_block(p, jf, near)], buf.at[at_block(p, jf, 2)], p["s"](turn))

    def gathered(p):
        for jf in range(SIDE):
            p["d"][jf][4 - turn_of[jf]].wait_recv()
            p["e"][jf].wait_recv()

    pair = {}

    def back_block(jz, jc):
        i = jz * 2 + jc
        wcopies[i].wait()
        target = psend if jc else ssum
        target[jz] = dot(g[...], wv[i], 1, 1).astype(BF16)
        if jc:
            pair[jz] = send(psend.at[jz], precv.at[jz], dev(flip=1))

    def pair_sum(jz):
        pair[jz].wait_recv()
        ssum[jz] = (ssum[jz].astype(F32) + precv[jz].astype(F32)).astype(BF16)

    def base_block(i, src, first=False):
        product = dot(src[...], wv[i], 1, 0)
        acc[...] = product if first else acc[...] + product

    def slots():
        names = index[...]
        slot = jnp.zeros_like(names)
        for a in range(SIDE * SIDE):
            slot = jnp.where(names == a, table[a], slot)
        return slot

    def project(p, rhs):
        gathered(p)
        full = dot(buf[pl.ds(p["base"], piece_rows), :], rhs[...], 1, 1)
        slot = slots()
        total = jnp.zeros((half, rows), F32)
        for jf in range(SIDE):
            for js in range(SIDE):
                first = (jf * SIDE + js) * half
                total = total + jnp.where(
                    slot == slot_of(p, jf, js), full[first : first + half, :], 0.0
                )
        small[p["i"]] = total

    sums = [{}, {}]

    def sum_pair(k):
        sums[k]["pair"] = send(small.at[2 * k + 1 - core], small_recv.at[k], dev(flip=1))

    def sum_far(k):
        sums[k]["pair"].wait_recv()
        small_sum[k] = small[2 * k + core] + small_recv[k]
        sums[k]["far"] = [
            send(small_sum.at[k], small_far.at[k, 3 - d], dev(dz=d)) for d in (2, 1, 3)
        ]

    def sum_back(k):
        for copy in sums[k]["far"]:
            copy.wait_recv()
        total = (small_sum[k] + small_far[k, 0]) + (small_far[k, 1] + small_far[k, 2])
        fin[2 * k + core] = ((SCALE if k else 1.0) * total).astype(BF16)
        sums[k]["last"] = send(fin.at[2 * k + core], fin.at[2 * k + core], dev(flip=1))

    def partial(p, jfs, rhs, scale):
        slot = slots()
        low = fin[(p["i"] + 2) % 4].astype(F32)
        for jf in jfs:
            for js in range(SIDE):
                lm[at_block(p, jf, js), :] = jnp.where(
                    slot == slot_of(p, jf, js), low, 0.0
                ).astype(BF16)
        group = pl.ds(p["base"] + jfs[0] * SIDE * half, len(jfs) * SIDE * half)
        part[group, :] = (scale * dot(lm[group, :], rhs[...], 1, 0)).astype(BF16)

    def reduce_first(p, jf):
        turn = turn_of[jf]
        i = p["i"]
        p["rh"][jf] = send(part.at[at_block(p, jf, 2)], r_half.at[i, jf], p["s"](turn))
        p["rf"][jf] = [
            send(part.at[at_block(p, jf, 4 - turn)], r_full.at[i, jf, 0], p["s"](4 - turn))
        ]

    def reduce_second(p, jf):
        turn = turn_of[jf]
        i = p["i"]
        p["rh"][jf].wait_recv()
        where = at_block(p, jf, turn)
        part[where, :] = (part[where, :].astype(F32) + r_half[i, jf].astype(F32)).astype(BF16)
        p["rf"][jf].append(send(part.at[where], r_full.at[i, jf, 1], p["s"](turn)))

    def collected(p, jf):
        i = p["i"]
        for copy in p["rf"][jf]:
            copy.wait_recv()
        total = r_full[i, jf, 0].astype(F32) + r_full[i, jf, 1].astype(F32)
        return part[at_block(p, jf, 0), :].astype(F32) + total

    def return_far(p):
        i = p["i"]
        red[i, 0] = collected(p, 2).astype(BF16)
        p["th"] = send(red.at[i, 0], t_half.at[i], p["f"](p["turn"]))

    def return_near(p):
        i, turn = p["i"], p["turn"]
        red[i, 1] = collected(p, 4 - turn).astype(BF16)
        p["tf"] = [send(red.at[i, 1], t_full.at[i, 0], p["f"](4 - turn))]

    def return_last(p):
        i, turn = p["i"], p["turn"]
        own = collected(p, turn)
        p["th"].wait_recv()
        red[i, 2] = (own + t_half[i].astype(F32)).astype(BF16)
        p["tf"].append(send(red.at[i, 2], t_full.at[i, 1], p["f"](turn)))

    def finish(p, out):
        i = p["i"]
        own = collected(p, 0)
        for copy in p["tf"]:
            copy.wait_recv()
        total = own + t_full[i, 0].astype(F32) + t_full[i, 1].astype(F32)
        out[pl.ds((i % 2) * half, half), :] = total.astype(BF16)

    a_pieces, b_pieces = pieces[:2], pieces[2:]
    top, bottom = pl.ds(0, mid), pl.ds(mid, mid)
    for p in pieces:
        p["rh"], p["rf"] = {}, {}

    def each(group, step, *args):
        for p in group:
            step(p, *args)

    a, c = a_pieces, b_pieces
    each(a, own_sends)
    x_up = [send(x.at[top], xs.at[6, top], dev(dz=1))]
    x_down = [send(x.at[bottom], xs.at[2, bottom], dev(dz=3))]
    x_up.append(send(x.at[bottom], xs.at[6, bottom], dev(dz=1)))
    x_down.append(send(x.at[top], xs.at[2, top], dev(dz=3)))
    x_pair = [send(x, xs.at[1], dev(flip=1))]
    back_block(2, 1)
    back_block(2, 0)
    each(pieces, keep_own)
    each(a, forward_first)
    each(c, own_sends)
    back_block(1, 1)
    each(a, forward_second, 0)
    each(a, first_far)
    each(a, forward_second, 1)
    each(a, forward_second, 3)
    x_up[0].wait_recv()
    x_far = [send(xs.at[6, top], xs.at[4, top], dev(dz=1))]
    x_down[0].wait_recv()
    x_far.append(send(xs.at[2, bottom], xs.at[4, bottom], dev(dz=3)))
    back_block(3, 1)
    each(a, forward_second, 2)
    each(c, forward_first)
    back_block(1, 0)
    each(c, forward_second, 0)
    each(a, project, x)
    sum_pair(0)
    each(c, first_far)
    sum_far(0)
    pair_sum(2)
    z_first = (
        send(ssum.at[2, top], z_half.at[0], dev(dz=1)),
        send(ssum.at[2, bottom], z_half.at[1], dev(dz=3)),
    )
    each(c, forward_second, 3)
    each(c, forward_second, 1)
    back_block(3, 0)
    sum_back(0)
    back_block(0, 1)
    each(c, forward_second, 2)
    sums[0]["last"].wait_recv()
    for jfs in ((2, 3), (0, 1)):
        for p in c:
            partial(p, jfs, g, SCALE)
            for jf in jfs:
                reduce_first(p, jf)
    each(c, project, g)
    sum_pair(1)
    x_up[1].wait_recv()
    x_pair.append(send(xs.at[6], xs.at[7], dev(flip=1)))
    x_down[1].wait_recv()
    x_pair.append(send(xs.at[2], xs.at[3], dev(flip=1)))
    x_far[0].wait_recv()
    x_far[1].wait_recv()
    x_pair.append(send(xs.at[4], xs.at[5], dev(flip=1)))
    each(c, reduce_second, 2)
    each(c, reduce_second, 3)
    sum_far(1)
    pair_sum(1)
    pair_sum(3)
    z_first[0].wait_recv()
    ssum[1, top] = (ssum[1, top].astype(F32) + z_half[0].astype(F32)).astype(BF16)
    z_second = [send(ssum.at[1], z_full.at[0], dev(dz=1))]
    z_first[1].wait_recv()
    ssum[3, bottom] = (ssum[3, bottom].astype(F32) + z_half[1].astype(F32)).astype(BF16)
    z_second.append(send(ssum.at[3], z_full.at[1], dev(dz=3)))
    each(c, reduce_second, 1)
    each(c, reduce_second, 0)
    back_block(0, 0)
    pair_sum(0)
    sum_back(1)
    each(c, return_far)
    sums[1]["last"].wait_recv()
    for jfs in ((2, 3), (0, 1)):
        for p in a:
            partial(p, jfs, x, 1.0)
            for jf in jfs:
                reduce_first(p, jf)
    each(c, return_near)
    base_block(0, x, first=True)
    base_block(6, xs.at[6])
    each(a, reduce_second, 2)
    each(c, return_last)
    base_block(2, xs.at[2])
    base_block(4, xs.at[4])
    for n, i in enumerate((1, 7)):
        x_pair[n].wait_recv()
        base_block(i, xs.at[i])
    each(a, reduce_second, 1)
    each(a, reduce_second, 3)
    each(a, return_far)
    each(a, reduce_second, 0)
    each(a, return_near)
    each(a, return_last)
    x_pair[2].wait_recv()
    base_block(3, xs.at[3])
    x_pair[3].wait_recv()
    base_block(5, xs.at[5])

    b_rows, a_rows = pl.ds(2 * piece_rows, 2 * piece_rows), pl.ds(0, 2 * piece_rows)
    term = (SCALE * dot(lm[b_rows, :], buf[b_rows, :], 0, 0)).astype(BF16)
    values[...] = (acc[...] + term.astype(F32)).astype(BF16)
    each(c, finish, d_expand)
    z_second[0].wait_recv()
    z_second[1].wait_recv()
    term = dot(lm[a_rows, :], buf[a_rows, :], 0, 0).astype(BF16)
    back = ssum[0].astype(F32) + z_full[0].astype(F32) + z_full[1].astype(F32)
    cotangent[...] = (back + term.astype(F32)).astype(BF16)
    each(a, finish, d_shrink)
    for copy in started:
        copy.wait_send()


def copy_out(*refs):
    half = len(refs) // 2
    sems = refs[-1]
    copies = [
        pltpu.make_async_copy(refs[i], refs[half + i], sems.at[i]) for i in range(half)
    ]
    for copy in copies:
        copy.start()
    for copy in copies:
        copy.wait()


def body(x, g, w, shrink, expand, index, table):
    rows, width = x.shape
    rank = expand.shape[1]
    slots = lax.axis_size("dp")
    vmem = pl.BlockSpec(memory_space=pltpu.VMEM)

    def scratch(*shape, dtype=BF16):
        return pltpu.VMEM(shape, dtype)

    out = pl.pallas_call(
        kernel,
        out_shape=(
            pltpu.VMEM((rows, width), BF16),
            pltpu.VMEM((rows, width), BF16),
            pltpu.VMEM((rank, width), BF16),
            pltpu.VMEM((rank, width), BF16),
        ),
        in_specs=[
            vmem,
            vmem,
            pl.BlockSpec(memory_space=pl.ANY),
            vmem,
            vmem,
            vmem,
            pl.BlockSpec(memory_space=pltpu.SMEM),
        ],
        out_specs=(vmem, vmem, vmem, vmem),
        scratch_shapes=[
            scratch(8, width, width),
            scratch(8, rows, width),
            scratch(2 * slots * rank, width),
            scratch(2 * slots * rank, width),
            scratch(4, rows, width),
            scratch(4, rows, width),
            scratch(4, rows, width),
            scratch(2, rows // 2, width),
            scratch(2, rows, width),
            scratch(rows, width, dtype=F32),
            scratch(4, rank // 2, rows, dtype=F32),
            scratch(2, rank // 2, rows, dtype=F32),
            scratch(2, rank // 2, rows, dtype=F32),
            scratch(2, 3, rank // 2, rows, dtype=F32),
            scratch(4, rank // 2, rows),
            scratch(2 * slots * rank, rows),
            scratch(4, 4, rank // 2, width),
            scratch(4, 4, 2, rank // 2, width),
            scratch(4, 3, rank // 2, width),
            scratch(4, rank // 2, width),
            scratch(4, 2, rank // 2, width),
            pltpu.SemaphoreType.DMA((8,)),
            pltpu.SemaphoreType.DMA((N_COPIES,)),
            pltpu.SemaphoreType.DMA((N_COPIES,)),
        ],
        compiler_params=pltpu.CompilerParams(
            collective_id=0, has_side_effects=True, vmem_limit_bytes=56 * 1024 * 1024
        ),
    )(x, g, w, shrink[0].T, expand[0], index.reshape(1, rows), table)
    anywhere = pl.BlockSpec(memory_space=pl.ANY)
    out = pl.pallas_call(
        copy_out,
        out_shape=[jax.ShapeDtypeStruct(o.shape, o.dtype) for o in out],
        in_specs=[vmem] * 4,
        out_specs=[anywhere] * 4,
        scratch_shapes=[pltpu.SemaphoreType.DMA((4,))],
    )(*[pltpu.with_memory_space_constraint(o, pltpu.VMEM) for o in out])
    return out[0], out[1], out[2].T[None], out[3][None]


def solution(mesh):
    return jax.shard_map(
        body,
        mesh=mesh,
        in_specs=(
            P("dp", "tensor"),
            P("dp", "tensor"),
            P(None, "tensor"),
            P("dp", "tensor", None),
            P("dp", None, "tensor"),
            P("dp", None),
            P(),
        ),
        out_specs=(
            P("dp", "tensor"),
            P("dp", "tensor"),
            P("dp", "tensor", None),
            P("dp", None, "tensor"),
        ),
        check_vma=False,
    )
```
